32 devices in a mesh: seq: 16 (over z, x, core), fsdp: 2 (over y).
Axes of the slice: x: 2, y: 2, z: 4, core: 2. Of those that a mesh axis runs over, the one named last changes fastest.
Arguments:
- tokens: bfloat16 [4096, 1024], P(('seq', 'fsdp')), may hold values from -32 to 32
- doc_bounds: int32 [2, 4096], P(None, ('seq', 'fsdp')), may hold values from 0 to 4096, as said below
- norm_one: bfloat16 [1024], P(('seq', 'fsdp')), may hold values from 0.099609375 to 1.8984375
- w_qkv: bfloat16 [1024, 3072], P(('seq', 'fsdp')), may hold values from -2 to 2
- w_out: bfloat16 [1024, 1024], P(('seq', 'fsdp')), may hold values from -1.5 to 1.5
- norm_two: bfloat16 [1024], P(('seq', 'fsdp')), may hold values from 0.099609375 to 1.8984375
- w_inner: bfloat16 [1024, 5248], P(('seq', 'fsdp')), may hold values from -0.1875 to 0.1875
- w_down: bfloat16 [1024, 2624], P(('seq', 'fsdp')), may hold values from -0.125 to 0.125
- cotangent: bfloat16 [4096, 1024], P(('seq', 'fsdp')), may hold values from -6 to 6
Outputs:
- layer_out: bfloat16 [4096, 1024], P(('seq', 'fsdp'))
- input_grad: float32 [4096, 1024], P(('seq', 'fsdp'))
- norm_one_grad: float32 [1024], P(('seq', 'fsdp'))
- qkv_grad: float32 [1024, 3072], P(('seq', 'fsdp'))
- out_grad: float32 [1024, 1024], P(('seq', 'fsdp'))
- norm_two_grad: float32 [1024], P(('seq', 'fsdp'))
- inner_grad: float32 [1024, 5248], P(('seq', 'fsdp'))
- down_grad: float32 [1024, 2624], P(('seq', 'fsdp'))
The draws below stay inside these ranges and needn't reach their ends.
Inputs may be any that keep to these rules, and one draw needn't show every extreme that they name: doc_bounds[0, i] and doc_bounds[1, i] are the first index and one past the last index of the document that holds token i; documents are contiguous runs of tokens that together cover all 4096 tokens of the packed stream.
All inputs are finite; a program needn't handle non-finite values.
Results may differ from the reference program's by a relative error of at most 0.014.
Values may be sent and summed in bfloat16 or wider, within the bound.
No kernel may reach another device: no remote copies, remote signals or barrier semaphores. Data moves between devices by JAX's collectives and lax.ppermute only.
A program may use at most 256 MiB of HBM per device.

```python
import math
import jax
import jax.numpy as jnp
from jax import lax

D = 1024
HEADS = 16
HEAD_DIM = 64
FF = 2624
W = 64
TOK_DEV = 128
TOKENS = 4096
SEQ_LEN = 4096


def draw_tokens(key, part):
    col_scale = jnp.exp(jax.random.uniform(jax.random.fold_in(key, 11), (1, D), jnp.float32, math.log(0.3), math.log(3.0)))
    row_scale = jnp.exp(jax.random.uniform(jax.random.fold_in(key, 12), (TOKENS, 1), jnp.float32, math.log(0.4), math.log(2.5)))
    base_draw = jnp.clip(jax.random.normal(jax.random.fold_in(key, 13), (TOKENS, D), jnp.float32), -4.0, 4.0)
    return (base_draw * col_scale * row_scale).astype(jnp.bfloat16)


def draw_w_qkv(key, part):
    base_draw = jnp.clip(jax.random.normal(jax.random.fold_in(key, 21), (D, 3 * D), jnp.float32), -5.0, 5.0) * D ** (-0.5)
    return base_draw.astype(jnp.bfloat16)


def draw_doc_bounds(key, part):
    position = jnp.arange(TOKENS, dtype=jnp.int32)
    flags = jax.random.randint(jax.random.fold_in(key, 31), (TOKENS,), 0, 4 * TOK_DEV) == 0
    flags = flags | (position % SEQ_LEN == 0)
    starts = lax.cummax(jnp.where(flags, position, 0), axis=0)
    marks = jnp.where(flags, position, TOKENS)
    shifted = jnp.concatenate([marks[1:], jnp.full((1,), TOKENS, jnp.int32)])
    ends = lax.cummin(shifted, axis=0, reverse=True)
    return jnp.stack([starts, ends]).astype(jnp.int32)


def with_spikes(values, stream_key, source, target, blocks, factor):
    def block_of(dim):
        return (jnp.arange(values.shape[dim]) // (values.shape[dim] // blocks)).reshape((-1,) + (1,) * (values.ndim - 1 - dim))

    first = jax.random.permutation(stream_key, blocks)[block_of(target)]
    second = (block_of(target) + blocks // 2) % blocks
    return jnp.where((block_of(source) == first) | (block_of(source) == second), factor * values, values)


def level_of(key, extent, pieces, low, largest):
    level = 1.0
    for axis_at, shards_of in pieces:
        draws = jax.random.uniform(jax.random.fold_in(jax.random.fold_in(key, 6), axis_at), (shards_of,), jnp.float32, low / len(pieces), largest / len(pieces))
        level = level * jnp.repeat(jnp.exp(draws), extent[axis_at] // shards_of).reshape((-1,) + (1,) * (len(extent) - 1 - axis_at))
    return level


def scatter_about(key, shape, scale, bound, split=(), held_as=jnp.bfloat16):
    result = jax.random.normal(key, shape, jnp.float32) * scale
    if len(split) > 0:
        result = level_of(key, shape, split, -0.22, 0.18) * result
    return jnp.clip(result, min=-bound, max=bound).astype(held_as)


def bell_draw_with(rng, shape, scale, bound, split, heavy, held_as=jnp.bfloat16):
    array = scale * jax.random.normal(rng, shape, jnp.float32)
    if split:
        array = array * level_of(rng, shape, split, -0.22, 0.18)
    return jnp.clip(with_spikes(array, jax.random.fold_in(rng, 3), *heavy), -bound, bound).astype(held_as)


def setup_inputs(seed: int = 0) -> dict:
    key_of = jax.random.split(jax.random.key(seed), 10)
    tokens = draw_tokens(jax.random.fold_in(key_of[9], 71), 0)
    doc_bounds = draw_doc_bounds(jax.random.fold_in(key_of[9], 71), 0)
    norm_one = jnp.clip(1.0 + 0.18 * jax.random.normal(key_of[2], (D,), jnp.float32), 0.099609375, 1.8984375).astype(jnp.bfloat16)
    w_qkv = draw_w_qkv(jax.random.fold_in(key_of[9], 71), 0)
    w_out = scatter_about(key_of[4], (D, D), (D // 64) ** -0.5, 1.5, ((0, 32),))
    norm_two = jnp.clip(1.0 + 0.18 * jax.random.normal(key_of[5], (D,), jnp.float32), 0.099609375, 1.8984375).astype(jnp.bfloat16)
    w_inner = scatter_about(key_of[6], (D, 2 * FF), D ** -0.5, 0.1875, ((0, 32),))
    w_down = scatter_about(key_of[7], (D, FF), FF ** -0.5, 0.125, ((0, 32),))
    cotangent = bell_draw_with(key_of[8], (TOKENS, D), 1.0, 6.0, ((0, 32),), (0, 1, 32, 2.75))
    return {"tokens": tokens, "doc_bounds": doc_bounds, "norm_one": norm_one, "w_qkv": w_qkv, "w_out": w_out, "norm_two": norm_two, "w_inner": w_inner, "w_down": w_down, "cotangent": cotangent}


EPS = 1e-05
THETA = 10000.0

def normalize(values):
    average = lax.optimization_barrier(jnp.mean(values, axis=1, keepdims=True))
    centred = values - average
    variance = lax.optimization_barrier(jnp.mean(centred * centred, axis=1, keepdims=True))
    inverse = lax.rsqrt(variance + EPS)
    return (centred * inverse, inverse)

def normalize_back(grad_rows, normed, inverse, gain):
    scaled = grad_rows * gain
    mean_plain = lax.optimization_barrier(jnp.mean(scaled, axis=1, keepdims=True))
    mean_cross = lax.optimization_barrier(jnp.mean(scaled * normed, axis=1, keepdims=True))
    return (inverse * (scaled - mean_plain - normed * mean_cross), lax.optimization_barrier(jnp.sum(grad_rows * normed, axis=0)))

def rotary_tables(positions):
    half_dim = HEAD_DIM // 2
    freqs = jnp.exp(-jnp.log(THETA) * 2.0 * jnp.arange(half_dim, dtype=jnp.float32) / HEAD_DIM)
    angles = positions[:, None] * freqs[None, :]
    return (jnp.cos(angles)[:, None, :], jnp.sin(angles)[:, None, :])

def rotate(values, cosine, sine):
    half_dim = HEAD_DIM // 2
    front_half = values[..., :half_dim]
    back_half = values[..., half_dim:]
    return jnp.concatenate([front_half * cosine - back_half * sine, back_half * cosine + front_half * sine], axis=-1)

def rotate_back(grads, cosine, sine):
    half_dim = HEAD_DIM // 2
    front_half = grads[..., :half_dim]
    back_half = grads[..., half_dim:]
    return jnp.concatenate([front_half * cosine + back_half * sine, back_half * cosine - front_half * sine], axis=-1)

def band_scores(queries, keys, visible):
    scores = jnp.einsum('qhd,khd->hqk', queries.astype(jnp.float32), keys.astype(jnp.float32)) * HEAD_DIM ** (-0.5)
    return jnp.where(visible[None], scores, -1e+30)

def attend(queries, keys, values, visible):
    scores = band_scores(queries, keys, visible)
    highest = lax.optimization_barrier(jnp.max(scores, axis=2, keepdims=True))
    summed = lax.optimization_barrier(jnp.sum(jnp.exp(scores - highest), axis=2, keepdims=True))
    log_total = highest + jnp.log(summed)
    weights = jnp.exp(scores - log_total).astype(jnp.bfloat16)
    mixed = jnp.einsum('hqk,khd->qhd', weights.astype(jnp.float32), values.astype(jnp.float32))
    return (mixed.astype(jnp.bfloat16), log_total)

def attend_back(queries, keys, values, mixed, grad_mixed, log_total, visible):
    scores = band_scores(queries, keys, visible)
    probs = jnp.exp(scores - log_total)
    weights = probs.astype(jnp.bfloat16)
    grad_probs = jnp.einsum('qhd,khd->hqk', grad_mixed.astype(jnp.float32), values.astype(jnp.float32))
    delta = jnp.transpose(lax.optimization_barrier(jnp.sum(grad_mixed.astype(jnp.float32) * mixed.astype(jnp.float32), axis=2)))[:, :, None]
    grad_scores = (probs * (grad_probs - delta)).astype(jnp.bfloat16).astype(jnp.float32)
    grad_queries = jnp.einsum('hqk,khd->qhd', grad_scores, keys.astype(jnp.float32)) * HEAD_DIM ** (-0.5)
    grad_keys = jnp.einsum('hqk,qhd->khd', grad_scores, queries.astype(jnp.float32)) * HEAD_DIM ** (-0.5)
    grad_values = jnp.einsum('hqk,qhd->khd', weights.astype(jnp.float32), grad_mixed.astype(jnp.float32))
    return (grad_queries, grad_keys, grad_values)

def reference(tokens, doc_bounds, norm_one, w_qkv, w_out, norm_two, w_inner, w_down, cotangent):
    total = tokens.shape[0]
    block = 512
    count = total // block
    inputs = tokens.astype(jnp.float32)
    gain_first = norm_one.astype(jnp.float32)
    gain_second = norm_two.astype(jnp.float32)
    normed_one, inverse_one = normalize(inputs)
    hidden_one = (normed_one * gain_first).astype(jnp.bfloat16)
    projected = jnp.dot(hidden_one, w_qkv, preferred_element_type=jnp.float32)
    token_index = jnp.arange(total, dtype=jnp.int32)
    starts = doc_bounds[0]
    ends = doc_bounds[1]
    cosine, sine = rotary_tables((token_index - starts).astype(jnp.float32))
    queries = rotate(projected[:, :D].reshape(total, HEADS, HEAD_DIM), cosine, sine).astype(jnp.bfloat16)
    keys = rotate(projected[:, D:2 * D].reshape(total, HEADS, HEAD_DIM), cosine, sine).astype(jnp.bfloat16)
    values = projected[:, 2 * D:].reshape(total, HEADS, HEAD_DIM).astype(jnp.bfloat16)
    pad_keys = jnp.pad(keys, ((W, W), (0, 0), (0, 0)))
    pad_values = jnp.pad(values, ((W, W), (0, 0), (0, 0)))

    def block_mask(first):
        query_index = first + jnp.arange(block, dtype=jnp.int32)
        key_index = first - W + jnp.arange(block + 2 * W, dtype=jnp.int32)
        start_rows = lax.dynamic_slice_in_dim(starts, first, block, 0)
        end_rows = lax.dynamic_slice_in_dim(ends, first, block, 0)
        near = jnp.abs(query_index[:, None] - key_index[None, :]) <= W
        inside = (key_index[None, :] >= start_rows[:, None]) & (key_index[None, :] < end_rows[:, None])
        return near & inside

    def forward_block(number):
        first = (number * block).astype(jnp.int32)
        query_rows = lax.dynamic_slice_in_dim(queries, first, block, 0)
        key_rows = lax.dynamic_slice_in_dim(pad_keys, first, block + 2 * W, 0)
        value_rows = lax.dynamic_slice_in_dim(pad_values, first, block + 2 * W, 0)
        return attend(query_rows, key_rows, value_rows, block_mask(first))
    numbers = jnp.arange(count, dtype=jnp.int32)
    mixed_blocks, log_totals = lax.map(forward_block, numbers)
    mixed = mixed_blocks.reshape(total, HEADS, HEAD_DIM)
    mixed_flat = mixed.reshape(total, D)
    residual = inputs + jnp.dot(mixed_flat, w_out, preferred_element_type=jnp.float32)
    normed_two, inverse_two = normalize(residual)
    hidden_two = (normed_two * gain_second).astype(jnp.bfloat16)
    inner = jnp.dot(hidden_two, w_inner, preferred_element_type=jnp.float32)
    gate_part = inner[:, :FF]
    upward = inner[:, FF:]
    normal_cdf = 0.5 * (1.0 + lax.erf(gate_part * 0.7071067811865476))
    activated = gate_part * normal_cdf
    product = (activated * upward).astype(jnp.bfloat16)
    layer_out = (residual + jnp.dot(product, w_down.T, preferred_element_type=jnp.float32)).astype(jnp.bfloat16)
    down_grad = jnp.dot(cotangent.T, product, preferred_element_type=jnp.float32)
    grad_product = jnp.dot(cotangent, w_down, preferred_element_type=jnp.float32)
    gate_slope = normal_cdf + gate_part * jnp.exp(-0.5 * gate_part * gate_part) * 0.3989422804014327
    grad_inner = jnp.concatenate([grad_product * upward * gate_slope, grad_product * activated], axis=1).astype(jnp.bfloat16)
    inner_grad = jnp.dot(hidden_two.T, grad_inner, preferred_element_type=jnp.float32)
    grad_hidden_two = jnp.dot(grad_inner, w_inner.T, preferred_element_type=jnp.float32)
    back_two, norm_two_grad = normalize_back(grad_hidden_two, normed_two, inverse_two, gain_second)
    grad_residual = cotangent.astype(jnp.float32) + back_two
    grad_res_low = grad_residual.astype(jnp.bfloat16)
    out_grad = jnp.dot(mixed_flat.T, grad_res_low, preferred_element_type=jnp.float32)
    grad_mixed = jnp.dot(grad_res_low, w_out.T, preferred_element_type=jnp.float32).astype(jnp.bfloat16)
    grad_mixed = grad_mixed.reshape(total, HEADS, HEAD_DIM)

    def backward_block(number, log_total):
        first = (number * block).astype(jnp.int32)
        query_rows = lax.dynamic_slice_in_dim(queries, first, block, 0)
        key_rows = lax.dynamic_slice_in_dim(pad_keys, first, block + 2 * W, 0)
        value_rows = lax.dynamic_slice_in_dim(pad_values, first, block + 2 * W, 0)
        mixed_rows = lax.dynamic_slice_in_dim(mixed, first, block, 0)
        grad_rows = lax.dynamic_slice_in_dim(grad_mixed, first, block, 0)
        return attend_back(query_rows, key_rows, value_rows, mixed_rows, grad_rows, log_total, block_mask(first))
    grad_q_blocks, grad_k_blocks, grad_v_blocks = lax.map(lambda pair: backward_block(pair[0], pair[1]), (numbers, log_totals))
    pair_grads = jnp.concatenate([grad_k_blocks.reshape(count, block + 2 * W, D), grad_v_blocks.reshape(count, block + 2 * W, D)], axis=2)
    own_grads = pair_grads[:, W:W + block]
    own_grads = own_grads.at[:-1, block - W:].add(pair_grads[1:, :W])
    own_grads = own_grads.at[1:, :W].add(pair_grads[:-1, W + block:])
    own_grads = own_grads.reshape(total, 2 * D)
    grad_q_raw = rotate_back(grad_q_blocks.reshape(total, HEADS, HEAD_DIM), cosine, sine).reshape(total, D)
    grad_k_raw = rotate_back(own_grads[:, :D].reshape(total, HEADS, HEAD_DIM), cosine, sine).reshape(total, D)
    grad_projected = jnp.concatenate([grad_q_raw, grad_k_raw, own_grads[:, D:]], axis=1).astype(jnp.bfloat16)
    qkv_grad = jnp.dot(hidden_one.T, grad_projected, preferred_element_type=jnp.float32)
    grad_hidden_one = jnp.dot(grad_projected, w_qkv.T, preferred_element_type=jnp.float32)
    back_one, norm_one_grad = normalize_back(grad_hidden_one, normed_one, inverse_one, gain_first)
    input_grad = grad_residual + back_one
    return (layer_out, input_grad, norm_one_grad, qkv_grad, out_grad, norm_two_grad, inner_grad, down_grad)
```

```python
import functools

import jax
import jax.numpy as jnp
from jax import lax
from jax.experimental import pallas as pl
from jax.experimental.pallas import tpu as pltpu
from jax.sharding import Mesh, PartitionSpec as P

HEAD_DIM = 64
W = 64
EPS = 1e-05
THETA = 10000.0
TP = 8
LANES = 128
ORDER = (0, 1, 4, 5, 2, 3, 6, 7)

bf16 = jnp.bfloat16
f32 = jnp.float32
PLANE = ("a", "c", "b")
ALL = ("g", "a", "c", "b")


def swap(value, axis):
    return lax.ppermute(value, axis, [(0, 1), (1, 0)])


def swap_both(value):
    return lax.ppermute(value, ("a", "b"), [(i, 3 - i) for i in range(4)])


def gather_plane(own):
    quad = [own, swap(own, "b"), swap(own, "a"), swap_both(own)]
    return jnp.concatenate(quad + [swap(q, "c") for q in quad], axis=0)


def scatter_plane(parts, rows):
    piece = [parts[i * rows : (i + 1) * rows] for i in range(TP)]
    pair = [piece[q].astype(f32) + swap(piece[4 + q], "c").astype(f32) for q in range(4)]
    return (
        pair[0]
        + swap(pair[1].astype(bf16), "b").astype(f32)
        + swap(pair[2].astype(bf16), "a").astype(f32)
        + swap_both(pair[3].astype(bf16)).astype(f32)
    )


def position_of(block, me):
    x = block ^ me
    return ((x >> 1) & 1) * 4 + ((x >> 2) & 1) * 2 + (x & 1)


def swap_halves(u):
    lane = lax.broadcasted_iota(jnp.int32, u.shape, 1)
    return jnp.where((lane & 63) < 32, pltpu.roll(u, 96, 1), pltpu.roll(u, 32, 1))


def project_body(x_ref, w_ref, cos_ref, sin_ref, n_ref, q_ref, k_ref, v_ref):
    x = x_ref[...].astype(f32)
    mean = jnp.mean(x, axis=1, keepdims=True)
    centred = x - mean
    var = jnp.mean(centred * centred, axis=1, keepdims=True)
    normed = (centred * lax.rsqrt(var + EPS)).astype(bf16)
    n_ref[...] = normed
    out = jnp.dot(normed, w_ref[...], preferred_element_type=f32)
    c = cos_ref[...]
    s = sin_ref[...]
    q = out[:, :LANES]
    k = out[:, LANES : 2 * LANES]
    q_ref[...] = (q * c + swap_halves(q) * s).astype(bf16)
    k_ref[...] = (k * c + swap_halves(k) * s).astype(bf16)
    v_ref[...] = out[:, 2 * LANES :].astype(bf16)


def project(x, w, cosine, sine, rows):
    total, dim = x.shape
    row = lambda i: (i, 0)
    lane_spec = pl.BlockSpec((rows, LANES), row)
    return pl.pallas_call(
        project_body,
        grid=(total // rows,),
        in_specs=[
            pl.BlockSpec((rows, dim), row),
            pl.BlockSpec((dim, 3 * LANES), lambda i: (0, 0)),
            lane_spec,
            lane_spec,
        ],
        out_specs=[pl.BlockSpec((rows, dim), row), lane_spec, lane_spec, lane_spec],
        out_shape=[jax.ShapeDtypeStruct((total, dim), bf16)]
        + [jax.ShapeDtypeStruct((total, LANES), bf16)] * 3,
        name="project",
    )(x, w, cosine, sine)


def fill_window(dst, src, before, after, me, rows):
    dst[0:W, :] = before
    for j in range(TP):
        at = pl.multiple_of(position_of(j, me) * rows, rows)
        dst[W + j * rows : W + (j + 1) * rows, :] = src[pl.ds(at, rows), :]
    dst[W + TP * rows : 2 * W + TP * rows, :] = after


def visible_of(st, en, first, rows):
    shape = (rows, rows + 2 * W)
    query = lax.broadcasted_iota(jnp.int32, shape, 0)
    key = lax.broadcasted_iota(jnp.int32, shape, 1)
    gap = key - query
    at = key + (first - W)
    return (gap >= 0) & (gap <= 2 * W) & (at >= st) & (at < en)


def keep_head(value, head):
    lane = lax.broadcasted_iota(jnp.int32, value.shape, 1)
    return jnp.where((lane >= HEAD_DIM) == (head == 1), value, jnp.zeros_like(value))


def pick_head(zero, one):
    lane = lax.broadcasted_iota(jnp.int32, (zero.shape[0], LANES), 1)
    return jnp.where(lane < HEAD_DIM, zero, one)


def dot_t(x, y):
    return lax.dot_general(x, y, (((1,), (1,)), ((), ())), preferred_element_type=f32)


def dot_rows(x, y):
    return lax.dot_general(x, y, (((0,), (0,)), ((), ())), preferred_element_type=f32)


def attend_body(rows, at_ref, q_ref, k_ref, v_ref, hb_ref, ha_ref, st_ref, en_ref, o_ref, l_ref, kw, vw):
    me = at_ref[0]
    base = at_ref[1]
    fill_window(kw, k_ref, hb_ref[:, :LANES], ha_ref[:, :LANES], me, rows)
    fill_window(vw, v_ref, hb_ref[:, LANES:], ha_ref[:, LANES:], me, rows)
    for j in range(TP):
        at = pl.multiple_of(position_of(j, me) * rows, rows)
        q = q_ref[pl.ds(at, rows), :]
        k = kw[j * rows : (j + 1) * rows + 2 * W, :]
        v = vw[j * rows : (j + 1) * rows + 2 * W, :]
        vis = visible_of(st_ref[pl.ds(at, rows), :], en_ref[pl.ds(at, rows), :], base + j * rows, rows)
        outs = []
        logs = []
        for h in range(2):
            s = jnp.where(vis, dot_t(keep_head(q, h), k) * HEAD_DIM ** (-0.5), -1e30)
            top = jnp.max(s, axis=1, keepdims=True)
            log_total = top + jnp.log(jnp.sum(jnp.exp(s - top), axis=1, keepdims=True))
            p = jnp.exp(s - log_total).astype(bf16)
            outs.append(jnp.dot(p, v, preferred_element_type=f32))
            logs.append(log_total)
        o_ref[pl.ds(at, rows), :] = pick_head(*outs).astype(bf16)
        l_ref[pl.ds(at, rows), :] = pick_head(*logs)


def attend(place, q, k, v, before, after, st, en, rows):
    total = q.shape[0]
    vm = pl.BlockSpec(memory_space=pltpu.VMEM)
    return pl.pallas_call(
        functools.partial(attend_body, rows),
        in_specs=[pl.BlockSpec(memory_space=pltpu.SMEM)] + [vm] * 7,
        out_specs=[vm, vm],
        out_shape=[jax.ShapeDtypeStruct((total, LANES), bf16), jax.ShapeDtypeStruct((total, LANES), f32)],
        scratch_shapes=[pltpu.VMEM((total + 2 * W, LANES), bf16)] * 2,
        name="attend",
    )(place, q, k, v, before, after, st, en)


def attend_back_body(
    rows, at_ref, q_ref, k_ref, v_ref, hb_ref, ha_ref, st_ref, en_ref, o_ref, l_ref, g_ref, cos_ref, sin_ref,
    dq_ref, dk_ref, dv_ref, kw, vw,
):
    me = at_ref[0]
    base = at_ref[1]
    fill_window(kw, k_ref, hb_ref[:, :LANES], ha_ref[:, :LANES], me, rows)
    fill_window(vw, v_ref, hb_ref[:, LANES:], ha_ref[:, LANES:], me, rows)
    dk_ref[...] = jnp.zeros_like(dk_ref)
    dv_ref[...] = jnp.zeros_like(dv_ref)
    scale = HEAD_DIM ** (-0.5)
    for j in range(TP):
        at = pl.multiple_of(position_of(j, me) * rows, rows)
        sl = slice(j * rows, (j + 1) * rows + 2 * W)
        q = q_ref[pl.ds(at, rows), :]
        k = kw[sl, :]
        v = vw[sl, :]
        g = g_ref[pl.ds(at, rows), :]
        both = g.astype(f32) * o_ref[pl.ds(at, rows), :].astype(f32)
        logs = l_ref[pl.ds(at, rows), :]
        vis = visible_of(st_ref[pl.ds(at, rows), :], en_ref[pl.ds(at, rows), :], base + j * rows, rows)
        dqs = []
        dk = jnp.zeros((rows + 2 * W, LANES), f32)
        dv = jnp.zeros((rows + 2 * W, LANES), f32)
        for h in range(2):
            qh = keep_head(q, h)
            gh = keep_head(g, h)
            s = jnp.where(vis, dot_t(qh, k) * scale, -1e30)
            p = jnp.exp(s - logs[:, h * HEAD_DIM : h * HEAD_DIM + 1])
            delta = jnp.sum(keep_head(both, h), axis=1, keepdims=True)
            ds = (p * (dot_t(gh, v) - delta)).astype(bf16)
            dqs.append(jnp.dot(ds, k, preferred_element_type=f32))
            dk = dk + dot_rows(ds, qh)
            dv = dv + dot_rows(p.astype(bf16), gh)
        dq = pick_head(*dqs) * scale
        c = cos_ref[pl.ds(at, rows), :]
        s = sin_ref[pl.ds(at, rows), :]
        dq_ref[pl.ds(at, rows), :] = (dq * c - swap_halves(dq) * s).astype(bf16)
        dk_ref[sl, :] += dk * scale
        dv_ref[sl, :] += dv


def attend_back(place, q, k, v, before, after, st, en, o, logs, g, cosine, sine, rows):
    total = q.shape[0]
    vm = pl.BlockSpec(memory_space=pltpu.VMEM)
    wide = jax.ShapeDtypeStruct((total + 2 * W, LANES), f32)
    return pl.pallas_call(
        functools.partial(attend_back_body, rows),
        in_specs=[pl.BlockSpec(memory_space=pltpu.SMEM)] + [vm] * 12,
        out_specs=[vm] * 3,
        out_shape=[jax.ShapeDtypeStruct((total, LANES), bf16), wide, wide],
        scratch_shapes=[pltpu.VMEM((total + 2 * W, LANES), bf16)] * 2,
        name="attend_back",
    )(place, q, k, v, before, after, st, en, o, logs, g, cosine, sine)


def finish_body(rows, at_ref, dq_ref, dk_ref, dv_ref, fb_ref, fa_ref, cos_ref, sin_ref, out_ref):
    me = at_ref[0]
    for j in range(TP):
        at = pl.multiple_of(position_of(j, me) * rows, rows)
        dk = dk_ref[W + j * rows : W + (j + 1) * rows, :]
        dv = dv_ref[W + j * rows : W + (j + 1) * rows, :]
        rest = jnp.zeros((rows - W, LANES), f32)
        if j == 0:
            both = fb_ref[...].astype(f32)
            dk = dk + jnp.concatenate([both[:, :LANES], rest], axis=0)
            dv = dv + jnp.concatenate([both[:, LANES:], rest], axis=0)
        if j == TP - 1:
            both = fa_ref[...].astype(f32)
            dk = dk + jnp.concatenate([rest, both[:, :LANES]], axis=0)
            dv = dv + jnp.concatenate([rest, both[:, LANES:]], axis=0)
        c = cos_ref[pl.ds(at, rows), :]
        s = sin_ref[pl.ds(at, rows), :]
        out_ref[pl.ds(at, rows), 0:LANES] = dq_ref[pl.ds(at, rows), :]
        out_ref[pl.ds(at, rows), LANES : 2 * LANES] = (dk * c - swap_halves(dk) * s).astype(bf16)
        out_ref[pl.ds(at, rows), 2 * LANES : 3 * LANES] = dv.astype(bf16)


def finish(place, dq, dk, dv, from_before, from_after, cosine, sine, rows):
    vm = pl.BlockSpec(memory_space=pltpu.VMEM)
    return pl.pallas_call(
        functools.partial(finish_body, rows),
        in_specs=[pl.BlockSpec(memory_space=pltpu.SMEM)] + [vm] * 7,
        out_specs=vm,
        out_shape=jax.ShapeDtypeStruct((dq.shape[0], 3 * LANES), bf16),
        name="finish",
    )(place, dq, dk, dv, from_before, from_after, cosine, sine)


def along(value, groups, by):
    return lax.ppermute(value, "g", [(i, i + by) for i in range(groups) if 0 <= i + by < groups])


def spread_groups(mine, groups):
    copies = jnp.broadcast_to(mine[None], (groups,) + mine.shape)
    got = lax.all_to_all(copies, "g", 0, 0, tiled=True)
    return got.reshape((groups * mine.shape[0],) + mine.shape[1:])


def columns_to_plane(blocks):
    got = lax.all_to_all(blocks, PLANE, 0, 0, tiled=True)
    return got.reshape((blocks.shape[0] * blocks.shape[1], blocks.shape[2]))


def layer_norm(values):
    average = jnp.mean(values, axis=1, keepdims=True)
    centred = values - average
    variance = jnp.mean(centred * centred, axis=1, keepdims=True)
    inverse = lax.rsqrt(variance + EPS)
    return (centred * inverse, inverse)


def layer_norm_back(scaled, normed, inverse):
    mean_plain = jnp.mean(scaled, axis=1, keepdims=True)
    mean_cross = jnp.mean(scaled * normed, axis=1, keepdims=True)
    return inverse * (scaled - mean_plain - normed * mean_cross)


def low_dot(x, y):
    return jnp.dot(x, y, preferred_element_type=f32)


def to_owners(grad, count, groups):
    own_rows, cols = grad.shape[0] // count, grad.shape[1]
    got = lax.all_to_all(grad.astype(bf16).reshape(count, own_rows, cols), ALL, 0, 0, tiled=True)
    return jnp.sum(got.reshape(groups, TP, own_rows, cols).astype(f32), axis=0)


def on_device(tokens, doc_bounds, norm_one, w_qkv, w_out, norm_two, w_inner, w_down, cotangent):
    rows, dim = tokens.shape
    own_rows = w_qkv.shape[0]
    ff = w_down.shape[1]
    groups = lax.axis_size("g")
    count = groups * TP
    group = lax.axis_index("g")
    me = lax.axis_index(PLANE)
    part = ff // TP
    wide = -(-part // LANES) * LANES
    base = group * (TP * rows)
    place = jnp.stack([me, base]).astype(jnp.int32)

    gain_one = norm_one.astype(f32)[:, None]
    gain_two = norm_two.astype(f32)[:, None]

    x_all = gather_plane(tokens)
    bounds = gather_plane(doc_bounds[None])
    qkv_mine = (w_qkv.astype(f32) * gain_one).astype(bf16).reshape(own_rows, 3, TP, LANES)
    qkv_mine = jnp.transpose(qkv_mine, (2, 0, 1, 3)).reshape(TP, own_rows, 3 * LANES)
    wq = spread_groups(columns_to_plane(qkv_mine), groups)

    def padded(mat):
        cut = jnp.transpose(mat.reshape(own_rows, TP, part), (1, 0, 2))
        return jnp.pad(cut, ((0, 0), (0, 0), (0, wide - part)))

    scaled_inner = (w_inner.astype(f32) * gain_two).astype(bf16)
    ff_mine = jnp.concatenate(
        [padded(scaled_inner[:, :ff]), padded(scaled_inner[:, ff:]), padded(w_down)], axis=2
    )
    wf = spread_groups(columns_to_plane(ff_mine), groups)
    w_both = wf[:, : 2 * wide]
    w_dn = wf[:, 2 * wide :]

    wo = jnp.zeros((own_rows * groups, dim), bf16)
    for k in range(groups):
        pairs = [(s, ((s % groups - k) % groups) * TP + s // groups) for s in range(count)]
        got = lax.ppermute(w_out, ALL, pairs)
        wo = lax.dynamic_update_slice(wo, got, (((group + k) % groups) * own_rows, 0))

    c_all = gather_plane(cotangent)

    start = bounds[:, 0, :].reshape(TP * rows, 1)
    end = bounds[:, 1, :].reshape(TP * rows, 1)
    slot = jnp.array(ORDER, jnp.int32)
    index = (base + (slot ^ me)[:, None] * rows + jnp.arange(rows, dtype=jnp.int32)[None, :]).reshape(TP * rows, 1)
    lane = jnp.arange(LANES, dtype=jnp.int32)
    half = HEAD_DIM // 2
    freqs = jnp.exp(-jnp.log(THETA) * 2.0 * (lane % half).astype(f32) / HEAD_DIM)
    angles = (index - start).astype(f32) * freqs[None, :]
    cosine = jnp.cos(angles)
    sine = jnp.sin(angles) * jnp.where(lane % HEAD_DIM < half, -1.0, 1.0)[None, :]

    n1, q, k, v = project(x_all, wq, cosine, sine, rows)
    at_first = position_of(0, me) * rows
    at_last = position_of(TP - 1, me) * rows + rows - W
    kv_first = jnp.concatenate([lax.dynamic_slice(t, (at_first, 0), (W, LANES)) for t in (k, v)], axis=1)
    kv_last = jnp.concatenate([lax.dynamic_slice(t, (at_last, 0), (W, LANES)) for t in (k, v)], axis=1)
    before = along(kv_last, groups, 1)
    after = along(kv_first, groups, -1)
    mixed, logs = attend(place, q, k, v, before, after, start, end, rows)
    inputs = tokens.astype(f32)
    residual = inputs + scatter_plane(low_dot(mixed, wo).astype(bf16), rows)
    normed_two, inverse_two = layer_norm(residual)
    n2 = gather_plane(normed_two.astype(bf16))

    inner = low_dot(n2, w_both)
    gate = inner[:, :wide]
    upward = inner[:, wide:]
    cdf = 0.5 * (1.0 + lax.erf(gate * 0.7071067811865476))
    activated = gate * cdf
    product = (activated * upward).astype(bf16)
    grad_product = low_dot(c_all, w_dn)
    slope = cdf + gate * jnp.exp(-0.5 * gate * gate) * 0.3989422804014327
    grad_inner = jnp.concatenate(
        [grad_product * upward * slope, grad_product * activated], axis=1
    ).astype(bf16)
    grad_scaled_two = scatter_plane(dot_t(grad_inner, w_both).astype(bf16), rows)
    layer_out = (residual + scatter_plane(dot_t(product, w_dn).astype(bf16), rows)).astype(bf16)
    ff_grad = to_owners(
        jnp.concatenate([dot_rows(n2, grad_inner).astype(bf16), dot_rows(c_all, product).astype(bf16)], axis=1),
        count,
        groups,
    )
    grad_residual = cotangent.astype(f32) + layer_norm_back(grad_scaled_two, normed_two, inverse_two)
    r_all = gather_plane(grad_residual.astype(bf16))

    grad_mixed = dot_t(r_all, wo).astype(bf16)
    dq, dk, dv = attend_back(place, q, k, v, before, after, start, end, mixed, logs, grad_mixed, cosine, sine, rows)
    pair = jnp.concatenate([dk, dv], axis=1)
    from_after = along(pair[:W].astype(bf16), groups, -1)
    from_before = along(pair[W + TP * rows :].astype(bf16), groups, 1)
    grad_projected = finish(place, dq, dk, dv, from_before, from_after, cosine, sine, rows)

    out_part = dot_rows(mixed, r_all).astype(bf16)
    out_grad = jnp.zeros((own_rows, dim), f32)
    for k_at in range(groups):
        pairs = [(z * TP + p, groups * p + (z + k_at) % groups) for z in range(groups) for p in range(TP)]
        cut = lax.dynamic_slice(out_part, (((group + k_at) % groups) * own_rows, 0), (own_rows, dim))
        out_grad = out_grad + lax.ppermute(cut, ALL, pairs).astype(f32)

    grad_scaled_one = scatter_plane(dot_t(grad_projected, wq).astype(bf16), rows)
    normed_one, inverse_one = layer_norm(inputs)
    input_grad = grad_residual + layer_norm_back(grad_scaled_one, normed_one, inverse_one)

    qkv_raw = to_owners(dot_rows(n1, grad_projected), count, groups)
    qkv_raw = jnp.transpose(qkv_raw.reshape(TP, own_rows, 3, LANES), (1, 2, 0, 3)).reshape(own_rows, 3 * dim)
    norm_one_grad = jnp.sum(qkv_raw * w_qkv.astype(f32), axis=1)
    qkv_grad = qkv_raw * gain_one

    def joined(at):
        cut = ff_grad[:, :, at * wide : at * wide + part]
        return jnp.transpose(cut, (1, 0, 2)).reshape(own_rows, ff)

    inner_raw = jnp.concatenate([joined(0), joined(1)], axis=1)
    norm_two_grad = jnp.sum(inner_raw * w_inner.astype(f32), axis=1)
    inner_grad = inner_raw * gain_two
    return (layer_out, input_grad, norm_one_grad, qkv_grad, out_grad, norm_two_grad, inner_grad, joined(2))


def solution(mesh):
    devices = mesh.devices.reshape(-1, 2, 2, 2)
    fine = Mesh(devices, ALL)
    row = P(ALL, None)
    vec = P(ALL)
    return jax.shard_map(
        on_device,
        mesh=fine,
        in_specs=(row, P(None, ALL), vec, row, row, vec, row, row, row),
        out_specs=(row, row, vec, row, row, vec, row, row),
        check_vma=False,
    )
```
